256 devices in a mesh: shot: 4 (over x_hi, core), space: 64 (over x_lo, y, z).
Axes of the slice: x: 4 (x_hi: 2, x_lo: 2; x = x_hi * 2 + x_lo), y: 4, z: 8, core: 2. Of those that a mesh axis runs over, the one named last changes fastest.
Arguments:
- residual_traces: float32 [4, 12, 16384], P('shot', None, 'space'), may hold values from -6 to 6
- owners: int32 [4, 16384, 1], P('shot', 'space'), may hold values from 0 to 63; in each aligned block of 256 rows (0 to 255, 256 to 511, ..., all dimensions but the last counted through in order) at most 8 rows name the same one
- surface_cells: int32 [4, 16384], P('shot', 'space'), may hold values from 0 to 511
- trace_counts: int32 [4], P('shot'), may hold values from 4096 to 16384, as said below
- start_current: float32 [4, 512, 64, 256], P('shot', 'space'), may hold values from -6 to 6
- start_later: float32 [4, 512, 64, 256], P('shot', 'space'), may hold values from -6 to 6
- forward_accel: bfloat16 [4, 12, 512, 64, 256], P('shot', None, 'space'), may hold values from -6 to 6
- courant_sq: float32 [512, 64, 256], P('space'), may hold values from 0.04 to 0.16
Outputs:
- adjoint_field: float32 [4, 512, 64, 256], P('shot', 'space')
- velocity_grad: float32 [512, 64, 256], P('space', 'shot')
The draws below stay inside these ranges and needn't reach their ends.
Inputs may be any that keep to these rules, and one draw needn't show every extreme that they name: `owners`: among the receivers of one device, no subdomain is named more than 8 times. `trace_counts`: some shot has all 16384 traces live.
All inputs are finite; a program needn't handle non-finite values.
Results may differ from the reference program's by a relative error of at most 0.0003.
Values sent between devices are 32-bit elements; how exact they have to be, the bound alone decides.
A program may use at most 64 MiB of HBM per device.

```python
import math
import jax
import jax.numpy as jnp
import numpy as np
from jax import lax

CX = 8
CY = 64
STEPS = 12
RECV_DEV = 256
CAP = 8
NSHOTS = 4
NX = 512
NY = 64
NZ = 256
RECV = 16384
N_SPACE = 64


def draw_trace_counts(key, part):
    first_key, second_key = jax.random.split(jax.random.fold_in(key, 17))
    values = jax.random.randint(first_key, (NSHOTS,), RECV // 4, RECV + 1)
    full_shot = jax.random.randint(second_key, (), 0, NSHOTS)
    return jnp.where(jnp.arange(NSHOTS) == full_shot, RECV, values).astype(jnp.int32)


def touch_ends(entries, own_key, smallest, largest):
    spot = [jax.random.randint(jax.random.fold_in(own_key, axis), (), 0, length) for axis, length in enumerate(entries.shape)]
    longest = entries.shape.index(max(entries.shape))
    beside = spot[:longest] + [(spot[longest] + 1) % entries.shape[longest]] + spot[longest + 1:]
    return entries.at[tuple(spot)].set(smallest).at[tuple(beside)].set(largest)


def block_scale(stream_key, shape, shards, smallest, top_value):
    gain = 1.0
    for axis_at, blocks in shards:
        draws = jax.random.uniform(jax.random.fold_in(jax.random.fold_in(stream_key, 6), axis_at), (blocks,), jnp.float32, smallest / len(shards), top_value / len(shards))
        gain = gain * jnp.repeat(jnp.exp(draws), shape[axis_at] // blocks).reshape((-1,) + (1,) * (len(shape) - 1 - axis_at))
    return gain


def shared_out(key, own, number, rows, number_of, top, limit, lean):
    sequence = jax.random.permutation(key, number_of)
    crowded, usual = shares(number_of, rows * top, limit, lean, True), shares(number_of, rows * top, limit, lean, False)
    places = jnp.arange(number_of)

    def named(sizes, turn):
        used = int((sizes > 0).sum())
        fixed = max(1, used // 4)
        passed = fixed + (places - fixed + turn * (used - fixed)) % max(1, number_of - fixed)
        return jnp.zeros((number_of,), jnp.int32).at[sequence[jnp.where(places < fixed, places, passed)]].set(jnp.asarray(sizes, jnp.int32))

    sizes = jnp.where(number % 4 == 0, named(crowded, number // 4), named(usual, number - number // 4 - 1))
    mixed = jax.random.permutation(jax.random.fold_in(own, 3), number_of)
    giver, sink = mixed[0:number_of // 2 * 2:2], mixed[1:number_of // 2 * 2:2]
    room = jnp.minimum(sizes[giver] - 1, limit - sizes[sink]) // 2
    room = jnp.where((giver == sequence[0]) | (sink == sequence[0]) | (sizes[sink] == 0), 0, jnp.maximum(room, 0))
    passed = jax.random.randint(jax.random.fold_in(own, 4), (number_of // 2,), 0, 1 << 20) % (room + 1)
    sizes = sizes.at[giver].add(-passed).at[sink].add(passed)
    labels = jnp.searchsorted(jnp.cumsum(sizes), jnp.arange(rows * top), side="right").astype(jnp.int32)
    listing = labels.reshape(top, rows).T
    listing = listing[jax.random.permutation(jax.random.fold_in(own, 1), rows)]
    turn = jax.random.randint(jax.random.fold_in(own, 2), (rows, 1), 0, top)
    return jnp.take_along_axis(listing, (jnp.arange(top)[None, :] + turn) % top, axis=1)


def shares(number_of, total, reach, slope, full):
    portions = [(1 << 20) // math.isqrt(rank ** slope) + 1 for rank in range(1, number_of + 1)]
    largest = reach if full else min(reach, max(-(-total // number_of), total * portions[0] // sum(portions)))
    least = 1 if total - largest >= number_of - 1 else 0
    counts, surplus = [largest] + [least] * (number_of - 1), total - largest - least * (number_of - 1)
    while surplus > 0:
        movable = [i for i in range(1, number_of) if counts[i] < largest] or [i for i in range(1, number_of) if counts[i] < reach]
        mass, remaining = sum([portions[i] for i in movable]), surplus
        for i in movable:
            addition = min(reach - counts[i], max(1, remaining * portions[i] // mass), surplus)
            counts[i] = counts[i] + addition
            surplus = surplus - addition
    return np.array(counts)


def scatter_about(rng, extent, width, bound, shards=(), kind=jnp.bfloat16):
    level = block_scale(rng, extent, shards, -0.22, 0.18) if shards else 1.0
    entries = jax.random.normal(rng, extent, jnp.float32) * width * level
    return jnp.minimum(jnp.maximum(entries, -bound), bound).astype(kind)


def setup_inputs(seed: int = 0) -> dict:
    key_list = jax.random.split(jax.random.key(seed), 9)
    residual_traces = scatter_about(key_list[0], (NSHOTS, STEPS, RECV), 1.0, 6.0, ((0, 4), (2, 64)), jnp.float32)
    owners_keys = jax.random.split(jax.random.fold_in(key_list[1], 1), NSHOTS * RECV // RECV_DEV)
    owners_turns = jax.random.permutation(jax.random.fold_in(key_list[1], 3), NSHOTS * RECV // RECV_DEV)
    owners = jax.vmap(lambda own, number: shared_out(jax.random.fold_in(key_list[1], 2), own, number, RECV_DEV, N_SPACE, 1, CAP, 2))(owners_keys, owners_turns).reshape((NSHOTS, RECV, 1))
    surface_cells = touch_ends(jax.random.randint(key_list[2], (NSHOTS, RECV), 0, CX * CY), jax.random.fold_in(key_list[2], 1), 0, (CX * CY) - 1).astype(jnp.int32)
    trace_counts = draw_trace_counts(jax.random.fold_in(key_list[8], 71), 0)
    start_current = scatter_about(key_list[4], (NSHOTS, NX, NY, NZ), 1.0, 6.0, ((0, 4), (1, 64)), jnp.float32)
    start_later = scatter_about(key_list[5], (NSHOTS, NX, NY, NZ), 1.0, 6.0, ((0, 4), (1, 64)), jnp.float32)
    forward_accel = scatter_about(key_list[6], (NSHOTS, STEPS, NX, NY, NZ), 1.0, 6.0, ((0, 4), (2, 64)))
    courant_sq = jnp.clip(jnp.exp(math.log(0.16) - 1.3862944 * jax.random.uniform(key_list[7], (NX, NY, NZ), jnp.float32) ** block_scale(key_list[7], (NX, NY, NZ), ((0, 64),), -0.2, 0.2)), 0.04, 0.16)
    return {"residual_traces": residual_traces, "owners": owners, "surface_cells": surface_cells, "trace_counts": trace_counts, "start_current": start_current, "start_later": start_later, "forward_accel": forward_accel, "courant_sq": courant_sq}


STENCIL_WEIGHTS = (-205.0 / 72.0, 8.0 / 5.0, -1.0 / 5.0, 8.0 / 315.0, -1.0 / 560.0)


def laplace(padded):
    length = padded.shape[0] - 8
    across = padded.shape[1] - 8
    height = padded.shape[2] - 8

    def window(off_x, off_y, off_z):
        return lax.slice(padded, (4 + off_x, 4 + off_y, 4 + off_z),
                         (4 + off_x + length, 4 + off_y + across, 4 + off_z + height))

    summed = (3.0 * STENCIL_WEIGHTS[0]) * window(0, 0, 0)
    for offset in range(1, 5):
        six_taps = window(offset, 0, 0) + window(-offset, 0, 0) + window(0, offset, 0)
        six_taps = six_taps + window(0, -offset, 0) + window(0, 0, offset) + window(0, 0, -offset)
        summed = summed + STENCIL_WEIGHTS[offset] * six_taps
    return summed


def one_shot(traces, owners, surface, live_count, first_field, prior_field, forward, courant_sq):
    number = jnp.arange(traces.shape[1], dtype=jnp.int32)
    weights = jnp.where((number < live_count)[None, :], traces, jnp.zeros_like(traces))
    row_x = owners[:, 0] * CX + surface // CY
    col_y = surface % CY
    planes = jnp.zeros((STEPS, NX, NY), jnp.float32).at[:, row_x, col_y].add(weights)
    current = first_field
    later = prior_field
    gradient = jnp.zeros((NX, NY, NZ), jnp.float32)
    for section in range(STEPS):
        fresh = 2.0 * current - later + courant_sq * laplace(jnp.pad(current, 4))
        fresh = fresh.at[:, :, 2].add(planes[section])
        gradient = gradient + fresh * forward[section].astype(jnp.float32)
        later, current = current, fresh
    return current, gradient


def reference(residual_traces, owners, surface_cells, trace_counts, start_current, start_later,
              forward_accel, courant_sq):
    fields = []
    gradients = []
    for shot_num in range(NSHOTS):
        current, gradient = one_shot(residual_traces[shot_num], owners[shot_num], surface_cells[shot_num],
                                     trace_counts[shot_num], start_current[shot_num], start_later[shot_num],
                                     forward_accel[shot_num], courant_sq)
        fields.append(current)
        gradients.append(gradient)
    summed = gradients[0]
    for extra in gradients[1:]:
        summed = summed + extra
    return jnp.stack(fields), summed
```

```python
import functools

import jax
import jax.numpy as jnp
from jax import lax
from jax.experimental import pallas as pl
from jax.experimental.pallas import tpu as pltpu
from jax.sharding import PartitionSpec as P

WEIGHTS = (-205.0 / 72.0, 8.0 / 5.0, -1.0 / 5.0, 8.0 / 315.0, -1.0 / 560.0)
REACH = 4
LANES = 128
PAD = 8
ROWS = 16
SLOTS = 8
FIELDS = 16
MESH = pl.DeviceIdType.MESH


def kernel(
    ring,
    blocks,
    traces,
    owners,
    cells,
    count,
    current_hbm,
    later_hbm,
    forward_hbm,
    courant_hbm,
    field_hbm,
    total_hbm,
    even,
    odd,
    courant,
    forward,
    gradient,
    listed,
    parted,
    along,
    turned,
    arrived,
    stacked,
    planes,
    from_core_x,
    from_core,
    from_x,
    load_sem,
    forward_sem,
    send_sem,
    recv_sem,
    along_sem,
    across_sem,
    sum_sem,
    out_sem,
):
    shot, space = lax.axis_index("shot"), lax.axis_index("space")
    last = ring * blocks - 1
    spot, block = lax.rem(space, ring), lax.div(space, ring)
    other_core = shot + 1 - 2 * lax.rem(shot, 2)
    other_x = lax.rem(shot + 2, 4)
    length, across, height = courant.shape
    steps, receivers = traces.shape
    own = slice(REACH, REACH + length)
    middle = slice(PAD, PAD + across)
    halves = [slice(0, LANES), slice(LANES, 2 * LANES)]

    loads = []
    for at, (source, target) in enumerate(((current_hbm, even), (later_hbm, odd))):
        for half in range(2):
            loads.append(
                pltpu.make_async_copy(
                    source.at[:, :, halves[half]],
                    target.at[own, half, middle, :],
                    load_sem.at[2 * at + half],
                )
            )
    loads.append(pltpu.make_async_copy(courant_hbm, courant, load_sem.at[4]))
    for load in loads:
        load.start()

    def forward_load(step):
        return pltpu.make_async_copy(
            forward_hbm.at[step], forward.at[step], forward_sem.at[step]
        )

    for field in (even, odd):
        zero = jnp.zeros((length, 2, PAD, LANES), jnp.float32)
        field[own, :, 0:PAD, :] = zero
        field[own, :, PAD + across : 2 * PAD + across, :] = zero

        @pl.when(space == 0)
        def _():
            field[0:REACH] = jnp.zeros((REACH,) + field.shape[1:], jnp.float32)

        @pl.when(space == last)
        def _():
            field[REACH + length :] = jnp.zeros((REACH,) + field.shape[1:], jnp.float32)

    gradient[...] = jnp.zeros_like(gradient)
    if ring * blocks < 64:
        along[...] = jnp.zeros_like(along)
        arrived[...] = jnp.zeros_like(arrived)

    barrier = pltpu.get_barrier_semaphore()

    def greet(**where):
        pl.semaphore_signal(barrier, inc=1, device_id=where, device_id_type=MESH)

    def ring_peer(offset):
        return lax.rem(spot + offset, ring)

    def block_peer(offset):
        return lax.rem(block + offset, blocks)

    @pl.when(space > 0)
    def _():
        greet(space=space - 1)

    @pl.when(space < last)
    def _():
        greet(space=space + 1)

    for offset in range(1, ring):
        greet(space=block * ring + ring_peer(offset))
    for offset in range(1, blocks):
        greet(space=block_peer(offset) * ring + spot)
    greet(shot=other_core)
    greet(shot=other_x)

    for step in range(steps):
        forward_load(step).start()

    row = lax.broadcasted_iota(jnp.int32, (64, receivers), 0)
    owner_of_row = (row & 7) * ring + (row >> 3)
    if ring * blocks < 64:
        real = ((row & 7) < blocks) & ((row >> 3) < ring)
        owner_of_row = jnp.where(real, owner_of_row, -1)
    hot = jnp.where(owners[...] == owner_of_row, 1.0, 0.0).astype(jnp.float32)
    earlier = jnp.where(
        lax.broadcasted_iota(jnp.int32, (receivers, receivers), 0)
        < lax.broadcasted_iota(jnp.int32, (receivers, receivers), 1),
        1.0,
        0.0,
    ).astype(jnp.float32)
    before = jnp.dot(hot, earlier, preferred_element_type=jnp.float32)
    rank = jnp.sum(hot * before, axis=0, keepdims=True).astype(jnp.int32)
    number = space * receivers + lax.broadcasted_iota(jnp.int32, (steps, receivers), 1)
    listed[...] = jnp.zeros_like(listed)
    listed[0:steps, :] = jnp.where(number < count[0], traces[...], 0.0)
    listed[steps : steps + 1, :] = cells[...].astype(jnp.float32)
    tiled = jnp.concatenate([listed[...]] * SLOTS, axis=0)
    slot = lax.broadcasted_iota(jnp.int32, tiled.shape, 0) >> 4
    placed = jnp.where(rank == slot, tiled, 0.0)
    parted[...] = lax.dot_general(
        hot,
        placed,
        (((1,), (1,)), ((), ())),
        precision=lax.Precision.HIGHEST,
        preferred_element_type=jnp.float32,
    ).reshape(parted.shape)

    ends = jnp.where(space == 0, 1, 0) + jnp.where(space == last, 1, 0)
    pl.semaphore_wait(barrier, ring + blocks + 2 - ends)

    def chunk_rows(place):
        chunk = (3 - shot, other_x, other_core, shot)[place]
        return pl.multiple_of(chunk * ROWS, ROWS)

    def halo(field, parity, place, way):
        rows = pl.ds(pl.multiple_of(PAD + chunk_rows(place), 8), ROWS)
        begin = (REACH, length)[way]
        end = (REACH + length, 0)[way]
        return pltpu.make_async_remote_copy(
            src_ref=field.at[begin : begin + REACH, :, rows, :],
            dst_ref=field.at[end : end + REACH, :, rows, :],
            send_sem=send_sem.at[parity, place, way],
            recv_sem=recv_sem.at[parity, place, way],
            device_id={"space": space + (-1, 1)[way]},
            device_id_type=MESH,
        )

    def sends(field, parity, place, wait):
        for way, there in ((0, space > 0), (1, space < last)):

            @pl.when(there)
            def _():
                copy = halo(field, parity, place, way)
                if wait:
                    copy.wait_send()
                else:
                    copy.start()

    def arrivals(field, parity, place):
        for way, there in ((0, space < last), (1, space > 0)):

            @pl.when(there)
            def _():
                halo(field, parity, place, way).wait_recv()

    def along_copy(offset):
        return pltpu.make_async_remote_copy(
            src_ref=parted.at[ring_peer(offset)],
            dst_ref=along.at[spot],
            send_sem=along_sem.at[0, offset],
            recv_sem=along_sem.at[1, offset],
            device_id={"space": block * ring + ring_peer(offset)},
            device_id_type=MESH,
        )

    for offset in range(1, ring):
        along_copy(offset).start()
    along[spot] = parted[spot]

    for load in loads[:2]:
        load.wait()
    for place in range(4):
        sends(even, 0, place, False)

    for offset in range(1, ring):
        along_copy(offset).wait_recv()
    for target in range(blocks):
        turned[target] = along[:, target, :]

    def across_copy(offset):
        return pltpu.make_async_remote_copy(
            src_ref=turned.at[block_peer(offset)],
            dst_ref=arrived.at[block],
            send_sem=across_sem.at[0, offset],
            recv_sem=across_sem.at[1, offset],
            device_id={"space": block_peer(offset) * ring + spot},
            device_id_type=MESH,
        )

    for offset in range(1, blocks):
        across_copy(offset).start()
    arrived[block] = turned[block]
    for load in loads[2:]:
        load.wait()
    for offset in range(1, blocks):
        across_copy(offset).wait_recv()

    rows64 = arrived[...].reshape(64, LANES)
    turned_rows = jnp.concatenate([rows64, jnp.zeros_like(rows64)], axis=0).T
    lane64 = lax.broadcasted_iota(jnp.int32, (64, LANES), 1)
    for at in range(SLOTS):
        moved = pltpu.roll(rows64, (LANES - at * FIELDS) % LANES, 1) if at else rows64
        moved = jnp.where(lane64 < FIELDS, moved, 0.0)
        high = moved.astype(jnp.bfloat16).astype(jnp.float32)
        rest = moved - high
        mid = rest.astype(jnp.bfloat16).astype(jnp.float32)
        low = rest - mid
        parts = high + pltpu.roll(mid, FIELDS, 1) + pltpu.roll(low, 2 * FIELDS, 1)
        begin = (at % 4) * LANES + (at // 4) * 64
        stacked[begin : begin + 64, :] = parts.astype(jnp.bfloat16)
    cell_rows = []
    for at in range(4):
        first = at * FIELDS + steps
        second = (at + 4) * FIELDS + steps
        cell_rows.append(
            turned_rows[first : first + 1, :]
            + pltpu.roll(turned_rows[second : second + 1, :], 64, 1)
        )
    cell_row = jnp.concatenate(cell_rows, axis=1).astype(jnp.int32)
    for at in range(4):
        cell = at * LANES + lax.broadcasted_iota(jnp.int32, (LANES, 4 * LANES), 0)
        table = jnp.where(cell == cell_row, 1.0, 0.0).astype(jnp.bfloat16)
        summed = jnp.dot(table, stacked[...], preferred_element_type=jnp.float32)
        summed = (
            summed
            + pltpu.roll(summed, LANES - FIELDS, 1)
            + pltpu.roll(summed, LANES - 2 * FIELDS, 1)
        )
        planes[at * LANES : (at + 1) * LANES, :] = summed

    lane = lax.broadcasted_iota(jnp.int32, (ROWS, LANES), 1)
    zeros = jnp.zeros((ROWS, LANES), jnp.float32)

    def compute(step, field, fresh_field, place):
        y = chunk_rows(place)
        rows = pl.ds(pl.multiple_of(PAD + y, 8), ROWS)
        flat = pl.ds(y, ROWS)
        for x in range(length):
            at = x + REACH
            centers = [field[at, half, rows, :] for half in range(2)]
            sums = [3.0 * WEIGHTS[0] * centers[half] for half in range(2)]
            for j in range(1, REACH + 1):
                up = [pltpu.roll(center, j, 1) for center in centers]
                down = [pltpu.roll(center, LANES - j, 1) for center in centers]
                z_taps = [
                    jnp.where(lane < j, zeros, up[0]) + jnp.where(lane < LANES - j, down[0], down[1]),
                    jnp.where(lane < j, up[0], up[1]) + jnp.where(lane < LANES - j, down[1], zeros),
                ]
                for half in range(2):
                    taps = field[at + j, half, rows, :] + field[at - j, half, rows, :]
                    taps = taps + field[at, half, pl.ds(PAD + y + j, ROWS), :]
                    taps = taps + field[at, half, pl.ds(PAD + y - j, ROWS), :]
                    sums[half] = sums[half] + WEIGHTS[j] * (taps + z_taps[half])
            for half in range(2):
                fresh = 2.0 * centers[half] - fresh_field[at, half, rows, :]
                fresh = fresh + courant[x, flat, halves[half]] * sums[half]
                if half == 0:
                    cell_at = pl.ds(pl.multiple_of(x * across + y, ROWS), ROWS)
                    source = pltpu.roll(planes[cell_at, :], lax.rem(LANES + 2 - step, LANES), 1)
                    fresh = fresh + jnp.where(lane == 2, source, 0.0)
                fresh_field[at, half, rows, :] = fresh
                accel = forward[step, x, flat, halves[half]].astype(jnp.float32)
                gradient[x, flat, halves[half]] += fresh * accel

    def reduce_copy(at, rows, target, peer):
        return pltpu.make_async_remote_copy(
            src_ref=gradient.at[:, rows, :],
            dst_ref=target,
            send_sem=sum_sem.at[0, at],
            recv_sem=sum_sem.at[1, at],
            device_id={"shot": peer},
            device_id_type=MESH,
        )

    def to_owner(place):
        target = (from_core_x, from_x, from_core)[place]
        peer = (other_core, other_x, other_core)[place]
        return reduce_copy(place, pl.ds(chunk_rows(place), ROWS), target, peer)

    def result_copies(place):
        y = chunk_rows(place)
        rows = pl.ds(pl.multiple_of(PAD + y, 8), ROWS)
        return [
            pltpu.make_async_copy(
                even.at[own, half, rows, :],
                field_hbm.at[:, pl.ds(y, ROWS), halves[half]],
                out_sem.at[2 * place + half],
            )
            for half in range(2)
        ]

    def two_steps(pair, carry):
        first, second = 2 * pair, 2 * pair + 1
        forward_load(first).wait()
        for place in range(4):
            arrivals(even, 0, place)

            @pl.when(pair > 0)
            def _():
                sends(odd, 1, place, True)

            compute(first, even, odd, place)
            sends(odd, 1, place, False)
        forward_load(second).wait()
        for place in range(4):
            arrivals(odd, 1, place)
            sends(even, 0, place, True)
            compute(second, odd, even, place)

            @pl.when(pair < steps // 2 - 1)
            def _():
                sends(even, 0, place, False)

            @pl.when(pair == steps // 2 - 1)
            def _():
                for copy in result_copies(place):
                    copy.start()
                if place == 1:
                    to_owner(0).wait_recv()
                    rows = pl.ds(chunk_rows(1), ROWS)
                    gradient[:, rows, :] += from_core_x[...]
                if place < 3:
                    to_owner(place).start()

        return carry

    lax.fori_loop(0, steps // 2, two_steps, 0)

    to_owner(2).wait_recv()
    rows = pl.ds(chunk_rows(3), ROWS)
    partial = gradient[:, rows, :] + from_core[...]
    to_owner(1).wait_recv()
    from_core[...] = partial + from_x[...]
    result = pltpu.make_async_copy(from_core, total_hbm, load_sem.at[0])
    result.start()
    for place in range(4):
        sends(odd, 1, place, True)
        for copy in result_copies(place):
            copy.wait()
    for place in range(3):
        to_owner(place).wait_send()
    for offset in range(1, ring):
        along_copy(offset).wait_send()
    for offset in range(1, blocks):
        across_copy(offset).wait_send()
    result.wait()


def shards(
    ring,
    blocks,
    residual_traces,
    owners,
    surface_cells,
    trace_counts,
    start_current,
    start_later,
    forward_accel,
    courant_sq,
):
    length, across, height = courant_sq.shape
    steps = residual_traces.shape[1]
    receivers = residual_traces.shape[2]
    field = pltpu.VMEM((length + 2 * REACH, 2, across + 2 * PAD, LANES), jnp.float32)
    piece = pltpu.VMEM((length, ROWS, height), jnp.float32)
    vmem = pl.BlockSpec(memory_space=pltpu.VMEM)
    anywhere = pl.BlockSpec(memory_space=pl.ANY)
    adjoint, total = pl.pallas_call(
        functools.partial(kernel, ring, blocks),
        out_shape=(
            jax.ShapeDtypeStruct((length, across, height), jnp.float32),
            jax.ShapeDtypeStruct((length, ROWS, height), jnp.float32),
        ),
        in_specs=[vmem, vmem, vmem, pl.BlockSpec(memory_space=pltpu.SMEM)] + [anywhere] * 4,
        out_specs=(anywhere, anywhere),
        scratch_shapes=[
            field,
            field,
            pltpu.VMEM((length, across, height), jnp.float32),
            pltpu.VMEM((steps, length, across, height), jnp.bfloat16),
            pltpu.VMEM((length, across, height), jnp.float32),
            pltpu.VMEM((FIELDS, receivers), jnp.float32),
            pltpu.VMEM((8, 8, LANES), jnp.float32),
            pltpu.VMEM((8, 8, LANES), jnp.float32),
            pltpu.VMEM((8, 8, LANES), jnp.float32),
            pltpu.VMEM((8, 8, LANES), jnp.float32),
            pltpu.VMEM((4 * LANES, LANES), jnp.bfloat16),
            pltpu.VMEM((length * across, LANES), jnp.float32),
            piece,
            piece,
            piece,
            pltpu.SemaphoreType.DMA((5,)),
            pltpu.SemaphoreType.DMA((steps,)),
            pltpu.SemaphoreType.DMA((2, 4, 2)),
            pltpu.SemaphoreType.DMA((2, 4, 2)),
            pltpu.SemaphoreType.DMA((2, 8)),
            pltpu.SemaphoreType.DMA((2, 8)),
            pltpu.SemaphoreType.DMA((2, 3)),
            pltpu.SemaphoreType.DMA((8,)),
        ],
        compiler_params=pltpu.CompilerParams(
            collective_id=0, has_side_effects=True, vmem_limit_bytes=60 * 2**20
        ),
    )(
        residual_traces[0],
        owners[0, :, 0][None, :],
        surface_cells,
        trace_counts,
        start_current[0],
        start_later[0],
        forward_accel[0],
        courant_sq,
    )
    return (adjoint[None], total)


def solution(mesh):
    placed = (
        P("shot", None, "space"),
        P("shot", "space", None),
        P("shot", "space"),
        P("shot"),
        P("shot", "space", None, None),
        P("shot", "space", None, None),
        P("shot", None, "space", None, None),
        P("space", None, None),
    )
    n_space = mesh.shape["space"]
    ring = 8 if n_space == 64 else 2
    return jax.shard_map(
        functools.partial(shards, ring, n_space // ring),
        mesh=mesh,
        in_specs=placed,
        out_specs=(P("shot", "space", None, None), P("space", "shot", None)),
        check_vma=False,
    )
```
